128 devices in a mesh: region: 4 (over x_lo, core), sector: 32 (over y, x_hi, z).
Axes of the slice: x: 4 (x_hi: 2, x_lo: 2; x = x_hi * 2 + x_lo), y: 4, z: 4, core: 2. Of those that a mesh axis runs over, the one named last changes fastest.
Arguments:
- env_left: bfloat16 [4, 8, 2048, 2048], P('region', None, 'sector'), may hold values from -6 to 6
- site_tensor: bfloat16 [4, 2048, 2, 2048], P('region', 'sector'), may hold values from -0.125 to 0.125
- mpo_tensor: float32 [4, 8, 8, 2, 2], P('region'), may hold values from -1 to 1
- env_right: bfloat16 [4, 8, 2048, 2048], P('region', None, 'sector'), may hold values from -0.046875 to 0.046875
- bond_tensor: bfloat16 [4, 2048, 2048], P('region'), may hold values from -0.125 to 0.125
Outputs:
- env_next: bfloat16 [4, 8, 2048, 2048], P('region', None, 'sector')
- bond_image: bfloat16 [4, 2048, 2048], P('region', 'sector')
The draws below stay inside these ranges and needn't reach their ends.
All inputs are finite; a program needn't handle non-finite values.
Results may differ from the reference program's by a relative error of at most 0.0065.
Values may be sent and summed in bfloat16 or wider, within the bound.
No kernel may reach another device: no remote copies, remote signals or barrier semaphores. Data moves between devices by JAX's collectives and lax.ppermute only.
A program may use at most 128 MiB of HBM per device.

```python
import jax
import jax.numpy as jnp
from jax import lax

CHI = 2048
W = 8
D_PHYS = 2
NREG = 4
N_REGION = 4


def level_of(own_key, dims, split, least, top_value):
    def one(position, shards_of):
        steps = jax.random.uniform(jax.random.fold_in(jax.random.fold_in(own_key, 6), position), (shards_of,), jnp.float32, least / len(split), top_value / len(split))
        return jnp.repeat(jnp.exp(steps), dims[position] // shards_of).reshape((-1,) + (1,) * (len(dims) - position - 1))

    factor_of = one(*split[0])
    for cut in split[1:]:
        factor_of = factor_of * one(*cut)
    return factor_of


def gaussian(rng, dims, scale, most, shards=(), dtype=jnp.bfloat16):
    values = jax.random.normal(rng, dims, jnp.float32) * scale
    if len(shards) > 0:
        values = level_of(rng, dims, shards, -0.22, 0.18) * values
    return jnp.clip(values, min=-most, max=most).astype(dtype)


def setup_inputs(seed: int = 0) -> dict:
    arg_keys = jax.random.split(jax.random.key(seed), 6)
    env_left = gaussian(arg_keys[0], (NREG, W, CHI, CHI), 1.0, 6.0, ((0, 4), (2, 32)))
    site_tensor = gaussian(arg_keys[1], (NREG, CHI, D_PHYS, CHI), CHI ** -0.5, 0.125, ((0, 4), (1, 32)))
    mpo_tensor = gaussian(arg_keys[2], (NREG, W, W, D_PHYS, D_PHYS), (W * D_PHYS * D_PHYS) ** -0.5, 1.0, ((0, 4),), jnp.float32)
    env_right = gaussian(arg_keys[3], (NREG, W, CHI, CHI), (CHI * W) ** -0.5, 0.046875, ((0, 4), (2, 32)))
    bond_tensor = gaussian(arg_keys[4], (NREG, CHI, CHI), CHI ** -0.5, 0.125, ((0, 4),))
    return dict(env_left=env_left, site_tensor=site_tensor, mpo_tensor=mpo_tensor, env_right=env_right, bond_tensor=bond_tensor)


def reference(env_left, site_tensor, mpo_tensor, env_right, bond_tensor):
    env_list = []
    image_list = []
    for region_id in range(N_REGION):
        site_whole = site_tensor[region_id].astype(jnp.float32)
        half_done = jnp.einsum("wak,ksc->wasc", env_left[region_id].astype(jnp.float32), site_whole)
        carried = jnp.einsum("vwst,vatc->wsac", mpo_tensor[region_id], half_done, precision=lax.Precision.HIGHEST).astype(jnp.bfloat16)
        env_new = jnp.einsum("wsac,asb->wcb", carried.astype(jnp.float32), site_whole).astype(jnp.bfloat16)
        right_next = env_right[(region_id + 1) % N_REGION].astype(jnp.float32)
        bond_right = jnp.einsum("wbc,kc->wbk", right_next, bond_tensor[region_id].astype(jnp.float32)).astype(jnp.bfloat16)
        image_new = jnp.einsum("wka,wbk->ab", env_new.astype(jnp.float32), bond_right.astype(jnp.float32)).astype(jnp.bfloat16)
        env_list.append(env_new)
        image_list.append(image_new)
    return jnp.stack(env_list), jnp.stack(image_list)
```

```python
import jax
import jax.numpy as jnp
from jax import lax
from jax.experimental import pallas as pl
from jax.experimental.pallas import tpu as pltpu
from jax.sharding import Mesh, PartitionSpec as P

F32, BF16 = jnp.float32, jnp.bfloat16
VMEM_LIMIT = 56 << 20


def hop(block, axis, distance):
    n = lax.axis_size(axis)
    return lax.ppermute(block, axis, [(i, (i + distance) % n) for i in range(n)])


def dot(a, b, dims):
    return lax.dot_general(a, b, (dims, ((), ())), preferred_element_type=F32)


def place(blocks, own, axis):
    shape = list(blocks[0].shape)
    shape[axis] = 4
    whole = jnp.zeros(shape, blocks[0].dtype)
    for distance, block in enumerate(blocks):
        start = [0] * len(shape)
        start[axis] = (own + distance) % 4
        whole = lax.dynamic_update_slice(whole, block, start)
    return whole


def gather_site(rows):
    y, x, z = (lax.axis_index(name) for name in ("y", "x", "z"))
    other = hop(rows, "x", 1)

    def both(state):
        pair = jnp.stack([rows[state], other[state]])
        return jnp.where(x == 0, pair, pair[::-1])[None, :, None]

    def around(block, axis):
        right, left = hop(block, axis, -1), hop(block, axis, 1)
        return right, hop(right[:, 0:1], axis, -1), hop(left[:, 1:2], axis, 1), left

    def line(block, axis, own, dim):
        right, far_0, far_1, left = around(block, axis)
        return place([block, right, jnp.concatenate([far_0, far_1], 1), left], own, dim)

    first, second = line(both(0), "z", z, 2), line(both(1), "y", y, 0)
    whole = jnp.zeros((4, 2, 4, 2) + rows.shape[1:], rows.dtype)

    def put(whole, block, yi, xi, zi, state):
        return lax.dynamic_update_slice(whole, block[:, :, :, None], (yi, xi, zi, state, 0, 0))

    whole = put(whole, first, y, 0, 0, 0)
    whole = put(whole, second, 0, 0, z, 1)
    right, far_0, far_1, left = around(first, "y")
    right_2, far_2, far_3, left_2 = around(second, "z")
    whole = put(whole, right, (y + 1) % 4, 0, 0, 0)
    whole = put(whole, left, (y + 3) % 4, 0, 0, 0)
    whole = put(whole, right_2, 0, 0, (z + 1) % 4, 1)
    whole = put(whole, left_2, 0, 0, (z + 3) % 4, 1)
    whole = put(whole, far_0, (y + 2) % 4, 0, 0, 0)
    whole = put(whole, far_1, (y + 2) % 4, 1, 0, 0)
    whole = put(whole, far_2, 0, 0, (z + 2) % 4, 1)
    whole = put(whole, far_3, 0, 1, (z + 2) % 4, 1)
    return whole.reshape((32, 2) + rows.shape[1:])


def bond_kernel(r_ref, b_ref, o_ref):
    rows = o_ref.shape[1]
    full = dot(r_ref[...], b_ref[...], ((1,), (1,)))
    low = lax.broadcasted_iota(jnp.int32, (rows, 128), 1) < 64
    for j in range(o_ref.shape[0] // 2):
        for w in range(full.shape[0] // rows // 2):
            a = full[2 * w * rows : (2 * w + 1) * rows, 128 * j : 128 * j + 128]
            b = full[(2 * w + 1) * rows : (2 * w + 2) * rows, 128 * j : 128 * j + 128]
            lanes = pl.ds(128 * w, 128)
            o_ref[2 * j, :, lanes] = jnp.where(low, a, pltpu.roll(b, 64, 1)).astype(BF16)
            o_ref[2 * j + 1, :, lanes] = jnp.where(low, pltpu.roll(a, 64, 1), b).astype(BF16)


def bond_right(right_next, bond):
    w, rows, c = right_next.shape
    k = bond.shape[0]
    tile = 256
    return pl.pallas_call(
        bond_kernel,
        out_shape=jax.ShapeDtypeStruct((k // 64, rows, w * 64), BF16),
        grid=(k // tile,),
        in_specs=[
            pl.BlockSpec((w * rows, c), lambda i: (0, 0)),
            pl.BlockSpec((tile, c), lambda i: (i, 0)),
        ],
        out_specs=pl.BlockSpec((tile // 64, rows, w * 64), lambda i: (i, 0, 0)),
        compiler_params=pltpu.CompilerParams(vmem_limit_bytes=VMEM_LIMIT),
        cost_estimate=pl.CostEstimate(flops=2 * w * rows * c * k, bytes_accessed=12 << 20, transcendentals=0),
        name="bond_right",
    )(right_next.reshape(w * rows, c), bond)


def absorb_kernel(m_ref, l_ref, g_ref, o_ref, h_ref):
    n, tile = l_ref.shape[1], g_ref.shape[3]
    w = o_ref.shape[1]
    rows = l_ref.shape[0] // w
    for t in range(2):
        h_ref[t] = dot(l_ref[...], g_ref[:, t].reshape(n, tile), ((1,), (0,)))
    for v in range(w):
        sums = []
        for s in range(2):
            total = None
            for u in range(w):
                for t in range(2):
                    term = m_ref[((u * w + v) * 2 + s) * 2 + t] * h_ref[t, u * rows : (u + 1) * rows, :]
                    total = term if total is None else total + term
            sums.append(total)
        turned = jnp.concatenate(sums, 0).T
        o_ref[:, v] = turned.reshape(tile // 64, 64, 2 * rows).astype(BF16)


def absorb(mpo, left, site):
    w, rows, k = left.shape
    columns = site.shape[3]
    tile = 256
    return pl.pallas_call(
        absorb_kernel,
        out_shape=jax.ShapeDtypeStruct((columns // 64, w, 64, 2 * rows), BF16),
        grid=(columns // tile,),
        in_specs=[
            pl.BlockSpec(memory_space=pltpu.SMEM),
            pl.BlockSpec((w * rows, k), lambda i: (0, 0)),
            pl.BlockSpec((32, 2, rows, tile), lambda i: (0, 0, 0, i)),
        ],
        out_specs=pl.BlockSpec((tile // 64, w, 64, 2 * rows), lambda i: (i, 0, 0, 0)),
        scratch_shapes=[pltpu.VMEM((2, w * rows, tile), F32)],
        compiler_params=pltpu.CompilerParams(vmem_limit_bytes=VMEM_LIMIT),
        cost_estimate=pl.CostEstimate(flops=4 * w * rows * k * columns, bytes_accessed=22 << 20, transcendentals=0),
        name="absorb",
    )(mpo.reshape(-1), left.reshape(w * rows, k), site)


def image_kernel(c_ref, g_ref, b_ref, e_ref, a_ref, z_ref, lhs_ref):
    parts, depth = c_ref.shape[0], c_ref.shape[2]

    @pl.when(pl.program_id(0) == 0)
    def _():
        for p in range(parts):
            lhs_ref[:, depth * p : depth * (p + 1)] = c_ref[p]

    env = dot(lhs_ref[...], g_ref[...], ((1,), (0,)))
    e_ref[...] = env.astype(BF16)
    turned = env.T.astype(BF16)
    half = b_ref.shape[0] // 2
    a_ref[0] = dot(turned, b_ref[:half, :], ((1,), (1,))).astype(BF16)
    z_ref[:, 0] = dot(turned, b_ref[half:, :], ((1,), (1,))).astype(BF16).reshape(4, 64, half)


def image(carried, site, bond):
    parts, rows, depth = carried.shape
    k, columns = site.shape
    tile = 256
    half = columns // 2
    return pl.pallas_call(
        image_kernel,
        out_shape=(
            jax.ShapeDtypeStruct((rows, columns), BF16),
            jax.ShapeDtypeStruct((columns // tile, tile, half), BF16),
            jax.ShapeDtypeStruct((4, columns // tile, 64, half), BF16),
        ),
        grid=(columns // tile,),
        in_specs=[
            pl.BlockSpec((parts, rows, depth), lambda i: (0, 0, 0)),
            pl.BlockSpec((k, tile), lambda i: (0, i)),
            pl.BlockSpec(bond.shape, lambda i: (0, 0)),
        ],
        out_specs=(
            pl.BlockSpec((rows, tile), lambda i: (0, i)),
            pl.BlockSpec((1, tile, half), lambda i: (i, 0, 0)),
            pl.BlockSpec((4, 1, 64, half), lambda i: (0, i, 0, 0)),
        ),
        scratch_shapes=[pltpu.VMEM((rows, parts * depth), BF16)],
        compiler_params=pltpu.CompilerParams(vmem_limit_bytes=VMEM_LIMIT),
        cost_estimate=pl.CostEstimate(flops=2 * rows * columns * (k + columns), bytes_accessed=32 << 20, transcendentals=0),
        name="image",
    )(carried, site, bond)


def pick(blocks, index):
    return lax.dynamic_index_in_dim(blocks, index, 0, keepdims=False)


def sum_line(blocks, axis):
    own = lax.axis_index(axis)
    half = blocks.shape[1] // 2
    right, far, left = (pick(blocks, (own + d) % 4) for d in (1, 2, 3))
    up = hop(far[:half], axis, 1)
    down = hop(far[half:], axis, -1)
    right_1 = hop(right[half:], axis, 1)
    left_0 = hop(left[:half], axis, -1)
    right_0 = hop((right[:half].astype(F32) + up.astype(F32)).astype(BF16), axis, 1)
    left_1 = hop((left[half:].astype(F32) + down.astype(F32)).astype(BF16), axis, -1)
    mine = pick(blocks, own).astype(F32)
    a = jnp.concatenate([right_0, right_1]).astype(F32)
    b = jnp.concatenate([left_0, left_1]).astype(F32)
    return mine + a + b


def sum_pair(blocks, axis):
    own = lax.axis_index(axis)
    theirs = hop(pick(blocks, 1 - own), axis, 1)
    return pick(blocks, own).astype(F32) + theirs.astype(F32)


def scatter_image(first, second):
    half = first.shape[-1]
    a = sum_line(first.reshape(4, 512, half), "y").astype(BF16)
    b = sum_line(second.reshape(4, 512, half), "z").astype(BF16)
    a = a.reshape(2, 4, 64, half).transpose(1, 0, 2, 3).reshape(4, 128, half)
    b = b.reshape(4, 128, half)
    a = sum_line(a, "z").astype(BF16)
    b = sum_line(b, "y").astype(BF16)
    both = jnp.concatenate([a, b], 1).reshape(2, 64, 2 * half)
    return sum_pair(both, "x").astype(BF16)


def local(env_left, site_tensor, mpo_tensor, env_right, bond_tensor):
    sector = ("y", "x", "z")
    route = [((i + 1) % 4, i) for i in range(4)]
    right_next = lax.ppermute(env_right, "region", route)[0]
    bond = bond_right(right_next, bond_tensor[0])
    site = gather_site(site_tensor[0].transpose(1, 0, 2))
    site, bond = lax.optimization_barrier((site, bond))
    bond = lax.all_to_all(bond, sector, split_axis=0, concat_axis=0, tiled=True)
    carried = absorb(mpo_tensor[0], env_left[0], site)
    carried = lax.all_to_all(carried, sector, split_axis=0, concat_axis=0, tiled=True)
    parts, w, columns, depth = carried.shape
    env_new, first, second = image(
        carried.reshape(parts, w * columns, depth),
        site.reshape(-1, site.shape[-1]),
        bond.reshape(-1, bond.shape[-1]),
    )
    return (
        env_new.reshape(1, w, columns, -1),
        scatter_image(first, second)[None],
    )


def solution(mesh):
    fine = Mesh(mesh.devices.reshape(4, 4, 2, 4), ("region", "y", "x", "z"))
    sector = ("y", "x", "z")
    return jax.shard_map(
        local,
        mesh=fine,
        in_specs=(
            P("region", None, sector, None),
            P("region", sector, None, None),
            P("region", None, None, None, None),
            P("region", None, sector, None),
            P("region", None, None),
        ),
        out_specs=(P("region", None, sector, None), P("region", sector, None)),
        check_vma=False,
    )
```

```python
import jax
import jax.numpy as jnp
from jax import lax
from jax.experimental import pallas as pl
from jax.experimental.pallas import tpu as pltpu
from jax.sharding import Mesh, PartitionSpec as P

F32, BF16 = jnp.float32, jnp.bfloat16
VMEM_LIMIT = 56 << 20


def hop(block, axis, distance):
    n = lax.axis_size(axis)
    return lax.ppermute(block, axis, [(i, (i + distance) % n) for i in range(n)])


def dot(a, b, dims):
    return lax.dot_general(a, b, (dims, ((), ())), preferred_element_type=F32)


def collect_kernel(at_ref, *refs):
    ins, outs, sem = refs[:16], refs[16:20], refs[20]
    x = at_ref[1]

    def copies(flip):
        made = []
        for state in range(2):
            own = at_ref[2] if state == 0 else at_ref[0]
            for n, (plane, distance) in enumerate([(p, d) for p in range(2) for d in range(4)]):
                where = outs[2 * state + (plane + flip) % 2].at[lax.rem(own + distance, 4)]
                made.append(pltpu.make_async_copy(ins[8 * state + n], where, sem.at[8 * state + n]))
        return made

    for flip in range(2):

        @pl.when(x == flip)
        def _():
            for copy in copies(flip):
                copy.start()
            for copy in copies(flip):
                copy.wait()


def collect(at, blocks):
    shape = jax.ShapeDtypeStruct((4,) + blocks[0].shape, blocks[0].dtype)
    anywhere = pl.BlockSpec(memory_space=pl.ANY)
    return pl.pallas_call(
        collect_kernel,
        out_shape=(shape,) * 4,
        in_specs=[pl.BlockSpec(memory_space=pltpu.SMEM)] + [anywhere] * 16,
        out_specs=(pl.BlockSpec(memory_space=pltpu.VMEM),) * 4,
        scratch_shapes=[pltpu.SemaphoreType.DMA((16,))],
        compiler_params=pltpu.CompilerParams(vmem_limit_bytes=16 << 20),
        cost_estimate=pl.CostEstimate(flops=0, bytes_accessed=8 << 20, transcendentals=0),
        name="collect",
    )(at, *blocks)


def around(near, other, axis):
    near_1, near_3 = hop(near, axis, -1), hop(near, axis, 1)
    other_3, other_1 = hop(other, axis, 1), hop(other, axis, -1)
    near_2 = hop(near_1, axis, -1)
    other_2 = hop(other_3, axis, 1)
    return [near, near_1, near_2, near_3, other, other_1, other_2, other_3]


def gather_site(at, rows):
    first, second = rows[0], rows[1]
    first_other, second_other = hop(first, "x", 1), hop(second, "x", 1)
    blocks = around(first, first_other, "z") + around(second, second_other, "y")
    a_0, a_1, b_0, b_1 = collect(at, blocks)
    return around(a_0, a_1, "y") + around(b_0, b_1, "z")


def site_copies(at_ref, blocks, buffer, sem, column, tile):
    made = []
    for n, (x, distance) in enumerate([(p, d) for p in range(2) for d in range(4)]):
        y, z = lax.rem(at_ref[0] + distance, 4), lax.rem(at_ref[2] + distance, 4)
        columns = pl.ds(pl.multiple_of(column, tile), tile)
        made.append(pltpu.make_async_copy(blocks[n].at[:, :, columns], buffer.at[y, x, :, 0], sem.at[n]))
        made.append(pltpu.make_async_copy(blocks[8 + n].at[:, :, columns], buffer.at[:, x, z, 1], sem.at[8 + n]))
    return made


def bond_kernel(r_ref, b_ref, o_ref):
    rows = o_ref.shape[1]
    full = dot(r_ref[...], b_ref[...], ((1,), (1,)))
    low = lax.broadcasted_iota(jnp.int32, (rows, 128), 1) < 64
    for j in range(o_ref.shape[0] // 2):
        for w in range(full.shape[0] // rows // 2):
            a = full[2 * w * rows : (2 * w + 1) * rows, 128 * j : 128 * j + 128]
            b = full[(2 * w + 1) * rows : (2 * w + 2) * rows, 128 * j : 128 * j + 128]
            lanes = pl.ds(128 * w, 128)
            o_ref[2 * j, :, lanes] = jnp.where(low, a, pltpu.roll(b, 64, 1)).astype(BF16)
            o_ref[2 * j + 1, :, lanes] = jnp.where(low, pltpu.roll(a, 64, 1), b).astype(BF16)


def bond_right(right_next, bond):
    w, rows, c = right_next.shape
    k = bond.shape[0]
    tile = 256
    return pl.pallas_call(
        bond_kernel,
        out_shape=jax.ShapeDtypeStruct((k // 64, rows, w * 64), BF16),
        grid=(k // tile,),
        in_specs=[
            pl.BlockSpec((w * rows, c), lambda i: (0, 0)),
            pl.BlockSpec((tile, c), lambda i: (i, 0)),
        ],
        out_specs=pl.BlockSpec((tile // 64, rows, w * 64), lambda i: (i, 0, 0)),
        compiler_params=pltpu.CompilerParams(vmem_limit_bytes=VMEM_LIMIT),
        cost_estimate=pl.CostEstimate(flops=2 * w * rows * c * k, bytes_accessed=12 << 20, transcendentals=0),
        name="bond_right",
    )(right_next.reshape(w * rows, c), bond)


def absorb_kernel(at_ref, m_ref, l_ref, *refs):
    blocks, o_ref, buffer, even_ref, odd_ref, sem = refs[:16], *refs[16:]
    tile, w = buffer.shape[-1], o_ref.shape[1]
    rows = l_ref.shape[0] // w
    i, last = pl.program_id(0), pl.num_programs(0) - 1

    def copies(step):
        slot = lax.rem(step, 2)
        return site_copies(at_ref, blocks, buffer.at[slot], sem.at[slot], step * tile, tile)

    @pl.when(i == 0)
    def _():
        for copy in copies(i):
            copy.start()

    @pl.when(i + 1 < last)
    def _():
        for copy in copies(i + 1):
            copy.start()

    @pl.when(i < last)
    def _():
        for copy in copies(i):
            copy.wait()

    def half(h_ref, slot):
        for t in range(2):
            site = buffer[slot, :, :, :, t].reshape(l_ref.shape[1], tile)
            h_ref[t] = dot(l_ref[...], site, ((1,), (0,)))

    def mix(h_ref):
        for v in range(w):
            sums = []
            for s in range(2):
                total = None
                for u in range(w):
                    for t in range(2):
                        term = m_ref[((u * w + v) * 2 + s) * 2 + t] * h_ref[t, u * rows : (u + 1) * rows, :]
                        total = term if total is None else total + term
                sums.append(total)
            turned = jnp.concatenate(sums, 0).T
            o_ref[:, v] = turned.reshape(tile // 64, 64, 2 * rows).astype(BF16)

    @pl.when(lax.rem(i, 2) == 0)
    def _():
        half(even_ref, 0)
        mix(odd_ref)

    @pl.when(lax.rem(i, 2) == 1)
    def _():
        half(odd_ref, 1)
        mix(even_ref)


def absorb(at, mpo, left, site):
    w, rows, k = left.shape
    columns = site[0].shape[-1]
    tile = 256
    scalars = pl.BlockSpec(memory_space=pltpu.SMEM)
    return pl.pallas_call(
        absorb_kernel,
        out_shape=jax.ShapeDtypeStruct((columns // 64, w, 64, 2 * rows), BF16),
        grid=(columns // tile + 1,),
        in_specs=[scalars, scalars, pl.BlockSpec((w * rows, k), lambda i: (0, 0))]
        + [pl.BlockSpec(memory_space=pl.ANY)] * 16,
        out_specs=pl.BlockSpec((tile // 64, w, 64, 2 * rows), lambda i: (jnp.maximum(i - 1, 0), 0, 0, 0)),
        scratch_shapes=[
            pltpu.VMEM((2, 4, 2, 4, 2, 64, tile), BF16),
            pltpu.VMEM((2, w * rows, tile), F32),
            pltpu.VMEM((2, w * rows, tile), F32),
            pltpu.SemaphoreType.DMA((2, 16)),
        ],
        compiler_params=pltpu.CompilerParams(vmem_limit_bytes=VMEM_LIMIT),
        cost_estimate=pl.CostEstimate(flops=4 * w * rows * k * columns, bytes_accessed=22 << 20, transcendentals=0),
        name="absorb",
    )(at, mpo.reshape(-1), left.reshape(w * rows, k), *site)


PIECES = (256, 256, 512, 512, 512)


def image_kernel(at_ref, c_ref, b_ref, *refs):
    blocks, e_ref, outs = refs[:16], refs[16], refs[17:27]
    buffer, lhs_ref, image_ref, sem, out_sem = refs[27:]
    parts, depth = c_ref.shape[0], c_ref.shape[2]
    tile = buffer.shape[-1]
    half = b_ref.shape[1] // 2
    i, count = pl.program_id(0), pl.num_programs(0)

    def copies(step):
        slot = lax.rem(step, 2)
        place = lax.rem(2 * at_ref[0] + step, count)
        return site_copies(at_ref, blocks, buffer.at[slot], sem.at[slot], place * tile, tile)

    def stores(step, static):
        slot = lax.rem(step, 2)
        src, done = image_ref.at[slot], out_sem.at[slot]
        place = lax.rem(2 * at_ref[0] + step, count)
        first = ((4, 0), (4, 256), (2, 0), (2, 256), (0, 0), (1, 0), (3, 0), (3, 256))[static]
        made = [pltpu.make_async_copy(src.at[0], outs[first[0]].at[pl.ds(first[1], tile)], done.at[0])]
        for piece, distance in ((2, 1), (3, 3), (4, 0)):
            rows = src.at[1, pl.ds(64 * lax.rem(at_ref[2] + distance, 4), 64)]
            made.append(pltpu.make_async_copy(rows, outs[5 + piece].at[place], done.at[piece]))
        far = src.at[1, pl.ds(64 * lax.rem(at_ref[2] + 2, 4), 64)]
        return made, far, place, done

    def each(step, act):
        for static in range(8):

            @pl.when(step == static)
            def _(static=static):
                made, far, place, done = stores(step, static)
                for copy in made:
                    act(copy)

                @pl.when(place < 4)
                def _():
                    act(pltpu.make_async_copy(far, outs[5].at[place], done.at[1]))

                @pl.when(place >= 4)
                def _():
                    act(pltpu.make_async_copy(far, outs[6].at[place - 4], done.at[1]))

    @pl.when(i == 0)
    def _():
        for copy in copies(i):
            copy.start()
        for p in range(parts):
            lhs_ref[:, depth * p : depth * (p + 1)] = c_ref[p]

    @pl.when(i + 1 < count)
    def _():
        for copy in copies(i + 1):
            copy.start()

    for copy in copies(i):
        copy.wait()

    slot = lax.rem(i, 2)
    env = dot(lhs_ref[...], buffer[slot].reshape(lhs_ref.shape[1], tile), ((1,), (0,)))
    e_ref[...] = env.astype(BF16)
    turned = env.T.astype(BF16)

    @pl.when(i >= 2)
    def _():
        each(i - 2, lambda copy: copy.wait())

    image_ref[slot, 0] = dot(turned, b_ref[:, :half], ((1,), (0,))).astype(BF16)
    image_ref[slot, 1] = dot(turned, b_ref[:, half:], ((1,), (0,))).astype(BF16)
    each(i, lambda copy: copy.start())

    @pl.when(i == count - 1)
    def _():
        each(i - 1, lambda copy: copy.wait())
        each(i, lambda copy: copy.wait())


def image(at, carried, site, bond):
    parts, rows, depth = carried.shape
    columns = site[0].shape[-1]
    tile, half = 256, columns // 2
    anywhere = pl.BlockSpec(memory_space=pl.ANY)
    grid = columns // tile
    return pl.pallas_call(
        image_kernel,
        out_shape=(
            jax.ShapeDtypeStruct((rows, columns), BF16),
            *(jax.ShapeDtypeStruct((n, half), BF16) for n in PIECES),
            *(jax.ShapeDtypeStruct((n // 64, 64, half), BF16) for n in PIECES),
        ),
        grid_spec=pltpu.PrefetchScalarGridSpec(
            num_scalar_prefetch=1,
            grid=(grid,),
            in_specs=[
                pl.BlockSpec((parts, rows, depth), lambda i, at: (0, 0, 0)),
                pl.BlockSpec(bond.shape, lambda i, at: (0, 0)),
            ]
            + [anywhere] * 16,
            out_specs=[pl.BlockSpec((rows, tile), lambda i, at: (0, lax.rem(2 * at[0] + i, grid)))] + [anywhere] * 10,
            scratch_shapes=[
                pltpu.VMEM((2, 4, 2, 4, 2, 64, tile), BF16),
                pltpu.VMEM((rows, parts * depth), BF16),
                pltpu.VMEM((2, 2, tile, half), BF16),
                pltpu.SemaphoreType.DMA((2, 16)),
                pltpu.SemaphoreType.DMA((2, 5)),
            ],
        ),
        compiler_params=pltpu.CompilerParams(vmem_limit_bytes=VMEM_LIMIT),
        cost_estimate=pl.CostEstimate(flops=2 * rows * columns * (parts * depth + columns), bytes_accessed=32 << 20, transcendentals=0),
        name="image",
    )(at, carried, bond, *site)


def add(*terms):
    total = terms[0].astype(F32)
    for term in terms[1:]:
        total = total + term.astype(F32)
    return total.astype(BF16)


def sum_line(far_low, far_high, right, left, own, axis):
    n = right.shape[0] // 2
    up, down = hop(far_low, axis, 1), hop(far_high, axis, -1)
    right_1, left_0 = hop(right[n:], axis, 1), hop(left[:n], axis, -1)
    right_0, left_1 = hop(add(right[:n], up), axis, 1), hop(add(left[n:], down), axis, -1)
    return jnp.concatenate([add(own[:n], right_0, left_0), add(own[n:], right_1, left_1)])


def sum_short(blocks, axis):
    own = lax.axis_index(axis)
    right, far, left, mine = (lax.dynamic_index_in_dim(blocks, (own + d) % 4, 0, keepdims=False) for d in (1, 2, 3, 0))
    return add(mine, hop(right, axis, 1), hop(left, axis, -1), hop(far, axis, 2))


def scatter_image(pieces):
    half = pieces[0].shape[-1]
    a = sum_line(*pieces[:5], "y")
    b = sum_line(*pieces[5:], "z")
    a = sum_short(a.reshape(2, 4, 64, half).transpose(1, 0, 2, 3), "z")
    b = sum_short(b.reshape(4, 2, 64, half), "y")
    both = jnp.concatenate([a, b], 2)
    own = lax.axis_index("x")
    theirs = hop(lax.dynamic_index_in_dim(both, 1 - own, 0, keepdims=False), "x", 1)
    return add(lax.dynamic_index_in_dim(both, own, 0, keepdims=False), theirs)


def local(env_left, site_tensor, mpo_tensor, env_right, bond_tensor):
    sector = ("y", "x", "z")
    at = jnp.stack([lax.axis_index(name) for name in sector]).astype(jnp.int32)
    route = [((i + 1) % 4, i) for i in range(4)]
    right_next = lax.ppermute(env_right, "region", route)[0]
    bond = bond_right(right_next, bond_tensor[0])
    site = gather_site(at, site_tensor[0].transpose(1, 0, 2))
    *site, bond = lax.optimization_barrier((*site, bond))
    bond = lax.all_to_all(bond, sector, split_axis=0, concat_axis=0, tiled=True)
    carried = absorb(at, mpo_tensor[0], env_left[0], site)
    carried = lax.all_to_all(carried, sector, split_axis=0, concat_axis=0, tiled=True)
    parts, w, columns, depth = carried.shape
    env_new, *pieces = image(
        at,
        carried.reshape(parts, w * columns, depth),
        site,
        bond.reshape(-1, bond.shape[-1]).T,
    )
    return (env_new.reshape(1, w, columns, -1), scatter_image(pieces)[None])


def solution(mesh):
    fine = Mesh(mesh.devices.reshape(4, 4, 2, 4), ("region", "y", "x", "z"))
    sector = ("y", "x", "z")
    return jax.shard_map(
        local,
        mesh=fine,
        in_specs=(
            P("region", None, sector, None),
            P("region", sector, None, None),
            P("region", None, None, None, None),
            P("region", None, sector, None),
            P("region", None, None),
        ),
        out_specs=(P("region", None, sector, None), P("region", sector, None)),
        check_vma=False,
    )
```

```python
import jax
import jax.numpy as jnp
from jax import lax
from jax.experimental import pallas as pl
from jax.experimental.pallas import tpu as pltpu
from jax.sharding import Mesh, PartitionSpec as P

F32, BF16 = jnp.float32, jnp.bfloat16
VMEM_LIMIT = 60 << 20


def hop(block, axis, distance):
    n = lax.axis_size(axis)
    return lax.ppermute(block, axis, [(i, (i + distance) % n) for i in range(n)])


def dot(a, b, dims):
    return lax.dot_general(a, b, (dims, ((), ())), preferred_element_type=F32)


def collect_kernel(at_ref, *refs):
    ins, outs, sem = refs[:16], refs[16:18], refs[18]
    copies = []
    for state in range(2):
        own = at_ref[2] if state == 0 else at_ref[0]
        for n, (plane, distance) in enumerate([(p, d) for p in range(2) for d in range(4)]):
            where = outs[state].at[lax.rem(plane + at_ref[1], 2), lax.rem(own + distance, 4)]
            copies.append(pltpu.make_async_copy(ins[8 * state + n], where, sem.at[8 * state + n]))
    for copy in copies:
        copy.start()
    for copy in copies:
        copy.wait()


def collect(at, blocks):
    shape = jax.ShapeDtypeStruct((2, 4) + blocks[0].shape, blocks[0].dtype)
    return pl.pallas_call(
        collect_kernel,
        out_shape=(shape,) * 2,
        in_specs=[pl.BlockSpec(memory_space=pltpu.SMEM)] + [pl.BlockSpec(memory_space=pl.ANY)] * 16,
        out_specs=(pl.BlockSpec(memory_space=pltpu.VMEM),) * 2,
        scratch_shapes=[pltpu.SemaphoreType.DMA((16,))],
        compiler_params=pltpu.CompilerParams(vmem_limit_bytes=VMEM_LIMIT),
        cost_estimate=pl.CostEstimate(flops=0, bytes_accessed=8 << 20, transcendentals=0),
        name="collect",
    )(at, *blocks)


def around(near, other, axis):
    near_1, near_3 = hop(near, axis, -1), hop(near, axis, 1)
    other_3, other_1 = hop(other, axis, 1), hop(other, axis, -1)
    near_2 = hop(near_1, axis, -1)
    other_2 = hop(other_3, axis, 1)
    return [near, near_1, near_2, near_3, other, other_1, other_2, other_3]


def halves_kernel(*refs):
    outs, sem = refs[-5:-1], refs[-1]
    copies = [pltpu.make_async_copy(refs[n].at[n % 2], outs[n], sem.at[n]) for n in range(4)]
    for copy in copies:
        copy.start()
    for copy in copies:
        copy.wait()


def halves(blocks, before):
    shape = jax.ShapeDtypeStruct(blocks[0].shape[1:], blocks[0].dtype)
    return pl.pallas_call(
        halves_kernel,
        out_shape=(shape,) * 4,
        in_specs=[pl.BlockSpec(memory_space=pl.ANY)] * (4 + len(before)),
        out_specs=(pl.BlockSpec(memory_space=pltpu.VMEM),) * 4,
        scratch_shapes=[pltpu.SemaphoreType.DMA((4,))],
        compiler_params=pltpu.CompilerParams(vmem_limit_bytes=VMEM_LIMIT),
        cost_estimate=pl.CostEstimate(flops=0, bytes_accessed=8 << 20, transcendentals=0),
        name="halves",
    )(*blocks, *before)


def gather_site(at, rows, before):
    first, second = rows[0], rows[1]
    first_other, second_other = hop(first, "x", 1), hop(second, "x", 1)
    a, b = collect(at, around(first, first_other, "z") + around(second, second_other, "y"))
    right_a, left_a, right_b, left_b = hop(a, "y", -1), hop(a, "y", 1), hop(b, "z", -1), hop(b, "z", 1)
    to_left_a, to_right_a, to_left_b, to_right_b = halves((right_a, left_a, right_b, left_b), before)
    return [
        *(a, right_a, left_a, hop(to_left_a, "y", -1), hop(to_right_a, "y", 1)),
        *(b, right_b, left_b, hop(to_left_b, "z", -1), hop(to_right_b, "z", 1)),
    ]


def site_copies(at_ref, blocks, buffer, sem, column, tile):
    made = []
    columns = pl.ds(pl.multiple_of(column, tile), tile)
    for x in range(2):
        for distance, place in ((0, 0), (1, 1), (3, 2), (2, 3 + x)):
            y, z = lax.rem(at_ref[0] + distance, 4), lax.rem(at_ref[2] + distance, 4)
            a, b = (ref if distance == 2 else ref.at[x] for ref in (blocks[place], blocks[5 + place]))
            n = 4 * x + distance
            made.append(pltpu.make_async_copy(a.at[:, :, columns], buffer.at[y, x, :, 0], sem.at[n]))
            made.append(pltpu.make_async_copy(b.at[:, :, columns], buffer.at[:, x, z, 1], sem.at[8 + n]))
    return made


def bond_kernel(r_ref, b_ref, o_ref):
    rows = o_ref.shape[1]
    full = dot(r_ref[...], b_ref[...], ((1,), (1,)))
    low = lax.broadcasted_iota(jnp.int32, (rows, 128), 1) < 64
    for j in range(o_ref.shape[0] // 2):
        for w in range(full.shape[0] // rows // 2):
            a = full[2 * w * rows : (2 * w + 1) * rows, 128 * j : 128 * j + 128]
            b = full[(2 * w + 1) * rows : (2 * w + 2) * rows, 128 * j : 128 * j + 128]
            lanes = pl.ds(128 * w, 128)
            o_ref[2 * j, :, lanes] = jnp.where(low, a, pltpu.roll(b, 64, 1)).astype(BF16)
            o_ref[2 * j + 1, :, lanes] = jnp.where(low, pltpu.roll(a, 64, 1), b).astype(BF16)


def bond_right(right_next, bond):
    w, rows, c = right_next.shape
    k = bond.shape[0]
    tile = 256
    return pl.pallas_call(
        bond_kernel,
        out_shape=jax.ShapeDtypeStruct((k // 64, rows, w * 64), BF16),
        grid=(k // tile,),
        in_specs=[
            pl.BlockSpec((w * rows, c), lambda i: (0, 0)),
            pl.BlockSpec((tile, c), lambda i: (i, 0)),
        ],
        out_specs=pl.BlockSpec((tile // 64, rows, w * 64), lambda i: (i, 0, 0)),
        compiler_params=pltpu.CompilerParams(vmem_limit_bytes=VMEM_LIMIT),
        cost_estimate=pl.CostEstimate(flops=2 * w * rows * c * k, bytes_accessed=12 << 20, transcendentals=0),
        name="bond_right",
    )(right_next.reshape(w * rows, c), bond)


def stacked(refs):
    return jnp.concatenate([ref[...].reshape(-1, ref.shape[-1]) for ref in refs], 0)


def begin_kernel(at_ref, first_ref, second_ref, *refs):
    blocks, h_ref, left_ref = refs[:6], refs[6], refs[7]

    @pl.when(pl.program_id(0) == 0)
    def _():
        for t, (source, own) in enumerate(((first_ref, at_ref[0]), (second_ref, at_ref[2]))):
            for n, distance in enumerate((0, 1, 3)):
                start = pl.multiple_of(512 * lax.rem(own + distance, 4), 512)
                left_ref[t, :, 512 * n : 512 * (n + 1)] = source[:, pl.ds(start, 512)]

    for t in range(2):
        h_ref[t] = dot(left_ref[t], stacked(blocks[3 * t : 3 * t + 3]), ((1,), (0,)))


def begin(at, first, second, blocks):
    rows, k = first.shape
    columns, tile = blocks[0].shape[-1], 256
    whole = pl.BlockSpec((rows, k), lambda i: (0, 0))
    return pl.pallas_call(
        begin_kernel,
        out_shape=jax.ShapeDtypeStruct((2, rows, columns), F32),
        grid=(columns // tile,),
        in_specs=[pl.BlockSpec(memory_space=pltpu.SMEM), whole, whole]
        + [pl.BlockSpec((2, 4, 64, tile), lambda i: (0, 0, 0, i))] * 6,
        out_specs=pl.BlockSpec((2, rows, tile), lambda i: (0, 0, i)),
        scratch_shapes=[pltpu.VMEM((2, rows, 3 * k // 4), BF16)],
        compiler_params=pltpu.CompilerParams(vmem_limit_bytes=VMEM_LIMIT),
        cost_estimate=pl.CostEstimate(flops=3 * rows * k * columns, bytes_accessed=24 << 20, transcendentals=0),
        name="begin",
    )(at, first, second, *blocks)


def hold(value, *before):
    anywhere = pl.BlockSpec(memory_space=pl.ANY)
    return pl.pallas_call(
        lambda *refs: None,
        out_shape=jax.ShapeDtypeStruct(value.shape, value.dtype),
        in_specs=[anywhere] * (1 + len(before)),
        out_specs=anywhere,
        input_output_aliases={0: 0},
        name="hold",
    )(value, *before)


def absorb_kernel(at_ref, m_ref, first_ref, second_ref, part_ref, *refs):
    blocks, o_ref, left_ref, h_ref = refs[:4], *refs[4:]
    w, tile = o_ref.shape[1], part_ref.shape[-1]
    rows = first_ref.shape[0] // w

    @pl.when(pl.program_id(0) == 0)
    def _():
        for t, (source, own) in enumerate(((first_ref, at_ref[0]), (second_ref, at_ref[2]))):
            left_ref[t] = source[:, pl.ds(pl.multiple_of(512 * lax.rem(own + 2, 4), 512), 512)]

    for t in range(2):
        h_ref[t] = part_ref[t] + dot(left_ref[t], stacked(blocks[2 * t : 2 * t + 2]), ((1,), (0,)))
    for v in range(w):
        sums = []
        for s in range(2):
            total = None
            for u in range(w):
                for t in range(2):
                    term = m_ref[((u * w + v) * 2 + s) * 2 + t] * h_ref[t, u * rows : (u + 1) * rows, :]
                    total = term if total is None else total + term
            sums.append(total)
        turned = jnp.concatenate(sums, 0).T
        o_ref[:, v] = turned.reshape(tile // 64, 64, 2 * rows).astype(BF16)


def absorb(at, mpo, first, second, part, blocks, w):
    rows, k = first.shape
    columns, tile = blocks[0].shape[-1], 256
    scalars = pl.BlockSpec(memory_space=pltpu.SMEM)
    whole = pl.BlockSpec((rows, k), lambda i: (0, 0))
    return pl.pallas_call(
        absorb_kernel,
        out_shape=jax.ShapeDtypeStruct((columns // 64, w, 64, 2 * rows // w), BF16),
        grid=(columns // tile,),
        in_specs=[scalars, scalars, whole, whole, pl.BlockSpec((2, rows, tile), lambda i: (0, 0, i))]
        + [pl.BlockSpec((4, 64, tile), lambda i: (0, 0, i))] * 4,
        out_specs=pl.BlockSpec((tile // 64, w, 64, 2 * rows // w), lambda i: (i, 0, 0, 0)),
        scratch_shapes=[pltpu.VMEM((2, rows, k // 4), BF16), pltpu.VMEM((2, rows, tile), F32)],
        compiler_params=pltpu.CompilerParams(vmem_limit_bytes=VMEM_LIMIT),
        cost_estimate=pl.CostEstimate(flops=rows * k * columns, bytes_accessed=20 << 20, transcendentals=0),
        name="absorb",
    )(at, mpo.reshape(-1), first, second, part, *blocks)


def step_kernel(at_ref, c_ref, *refs):
    blocks, e_ref, t_ref = refs[:10], refs[10], refs[11]
    buffer, lhs_ref, sem, lhs_sem = refs[12:]
    parts, depth = c_ref.shape[0], c_ref.shape[2]
    tile = buffer.shape[-1]
    i, count = pl.program_id(0), pl.num_programs(0)

    def copies(step):
        slot = lax.rem(step, 2)
        return site_copies(at_ref, blocks, buffer.at[slot], sem.at[slot], step * tile, tile)

    def sides():
        return [
            pltpu.make_async_copy(c_ref.at[p], lhs_ref.at[:, pl.ds(depth * p, depth)], lhs_sem.at[p])
            for p in range(parts)
        ]

    @pl.when(i == 0)
    def _():
        for copy in sides() + copies(i):
            copy.start()

    @pl.when(i + 1 < count)
    def _():
        for copy in copies(i + 1):
            copy.start()

    @pl.when(i == 0)
    def _():
        for copy in sides():
            copy.wait()

    for copy in copies(i):
        copy.wait()
    env = dot(lhs_ref[...], buffer[lax.rem(i, 2)].reshape(lhs_ref.shape[1], tile), ((1,), (0,)))
    e_ref[...] = env.astype(BF16)
    t_ref[...] = env.T.astype(BF16)


def step(at, carried, site):
    parts, rows, depth = carried.shape
    columns, tile = site[0].shape[-1], 256
    anywhere = pl.BlockSpec(memory_space=pl.ANY)
    return pl.pallas_call(
        step_kernel,
        out_shape=(jax.ShapeDtypeStruct((rows, columns), BF16), jax.ShapeDtypeStruct((columns, rows), BF16)),
        grid=(columns // tile,),
        in_specs=[pl.BlockSpec(memory_space=pltpu.SMEM)] + [anywhere] * 11,
        out_specs=(pl.BlockSpec((rows, tile), lambda i: (0, i)), pl.BlockSpec((tile, rows), lambda i: (i, 0))),
        scratch_shapes=[
            pltpu.VMEM((2, 4, 2, 4, 2, 64, tile), BF16),
            pltpu.VMEM((rows, parts * depth), BF16),
            pltpu.SemaphoreType.DMA((2, 16)),
            pltpu.SemaphoreType.DMA((parts,)),
        ],
        compiler_params=pltpu.CompilerParams(vmem_limit_bytes=VMEM_LIMIT),
        cost_estimate=pl.CostEstimate(flops=2 * rows * columns * parts * depth, bytes_accessed=24 << 20, transcendentals=0),
        name="step",
    )(at, carried, *site)


def terms_kernel(distances, at_ref, t_ref, b_ref, *outs):
    half = b_ref.shape[1] // 2
    n = len(distances)
    for m, distance in enumerate(distances):
        y, z = lax.rem(at_ref[0] + distance, 4), lax.rem(at_ref[2] + distance, 4)
        for side in range(2):
            for part in range(2):
                if side == 0:
                    rows = t_ref[pl.ds(2 * y + part, 1), :].reshape(256, -1)
                else:
                    rows = t_ref[4 * part : 4 * part + 4, pl.ds(z, 1)].reshape(256, -1)
                columns = b_ref[:, half * side : half * (side + 1)]
                outs[2 * n * side + 2 * m + part][...] = dot(rows, columns, ((1,), (0,))).astype(BF16)


def terms(distances, at, turned, bond):
    depth, columns = bond.shape
    half = columns // 2
    vmem = pl.BlockSpec(memory_space=pltpu.VMEM)
    count = 4 * len(distances)
    return pl.pallas_call(
        lambda *refs: terms_kernel(distances, *refs),
        out_shape=(jax.ShapeDtypeStruct((256, half), BF16),) * count,
        in_specs=[pl.BlockSpec(memory_space=pltpu.SMEM), vmem, vmem],
        out_specs=(vmem,) * count,
        compiler_params=pltpu.CompilerParams(vmem_limit_bytes=24 << 20),
        cost_estimate=pl.CostEstimate(flops=count * 2 * 256 * half * depth, bytes_accessed=count << 19, transcendentals=0),
        name="terms_%d" % len(distances),
    )(at, turned.reshape(8, 4, 64, depth), bond)


def add(*terms):
    total = terms[0].astype(F32)
    for term in terms[1:]:
        total = total + term.astype(F32)
    return total.astype(BF16)


def sum_line(far, right, left, own, axis):
    up, down = hop(far[0], axis, 1), hop(far[1], axis, -1)
    right = hop(jnp.stack([add(right[0], up), right[1]]), axis, 1)
    left = hop(jnp.stack([left[0], add(left[1], down)]), axis, -1)
    return add(jnp.stack(own), right, left)


def sum_short(blocks, axis):
    own = lax.axis_index(axis)
    right, far, left, mine = (lax.dynamic_index_in_dim(blocks, (own + d) % 4, 0, keepdims=False) for d in (1, 2, 3, 0))
    return add(mine, hop(right, axis, 1), hop(left, axis, -1), hop(far, axis, 2))


def scatter_image(far, rest):
    half = far[0].shape[-1]
    a = sum_line(far[:2], rest[0:2], rest[2:4], rest[4:6], "y")
    b = sum_line(far[2:], rest[6:8], rest[8:10], rest[10:12], "z")
    a = sum_short(a.reshape(2, 4, 64, half).transpose(1, 0, 2, 3), "z")
    b = sum_short(b.reshape(4, 2, 64, half), "y")
    both = jnp.concatenate([a, b], 2)
    own = lax.axis_index("x")
    theirs = hop(lax.dynamic_index_in_dim(both, 1 - own, 0, keepdims=False), "x", 1)
    return add(lax.dynamic_index_in_dim(both, own, 0, keepdims=False), theirs)


def local(env_left, site_tensor, mpo_tensor, env_right, bond_tensor):
    sector = ("y", "x", "z")
    at = jnp.stack([lax.axis_index(name) for name in sector]).astype(jnp.int32)
    route = [((i + 1) % 4, i) for i in range(4)]
    right_next = lax.ppermute(env_right, "region", route)[0]
    bond = bond_right(right_next, bond_tensor[0])
    w, rows, k = env_left.shape[1:]
    first = env_left.reshape(w * rows, k)
    second = first.reshape(w * rows, 4, 2, 4, 64).transpose(0, 3, 2, 1, 4).reshape(w * rows, k)
    site = gather_site(at, site_tensor[0].transpose(1, 0, 2), (bond, second))
    near, far = site[0:3] + site[5:8], site[3:5] + site[8:10]
    part = begin(at, first, second, near)
    bond = hold(bond, part, *site)
    bond = lax.all_to_all(bond, sector, split_axis=0, concat_axis=0, tiled=True)
    carried = absorb(at, mpo_tensor[0], first, second, part, far, w)
    carried = lax.all_to_all(carried, sector, split_axis=0, concat_axis=0, tiled=True)
    parts, w, columns, depth = carried.shape
    env_new, turned = step(at, carried.reshape(parts, w * columns, depth), site)
    bond = bond.reshape(-1, bond.shape[-1]).T
    far_terms = terms((2,), at, turned, bond)
    rest_terms = terms((1, 3, 0), at, turned, bond)
    return (env_new.reshape(1, w, columns, -1), scatter_image(far_terms, rest_terms)[None])


def solution(mesh):
    fine = Mesh(mesh.devices.reshape(4, 4, 2, 4), ("region", "y", "x", "z"))
    sector = ("y", "x", "z")
    return jax.shard_map(
        local,
        mesh=fine,
        in_specs=(
            P("region", None, sector, None),
            P("region", sector, None, None),
            P("region", None, None, None, None),
            P("region", None, sector, None),
            P("region", None, None),
        ),
        out_specs=(P("region", None, sector, None), P("region", sector, None)),
        check_vma=False,
    )
```

```python
import jax
import jax.numpy as jnp
from jax import lax
from jax.experimental import pallas as pl
from jax.experimental.pallas import tpu as pltpu
from jax.sharding import Mesh, PartitionSpec as P

F32, BF16 = jnp.float32, jnp.bfloat16
VMEM_LIMIT = 60 << 20


def hop(block, axis, distance):
    n = lax.axis_size(axis)
    return lax.ppermute(block, axis, [(i, (i + distance) % n) for i in range(n)])


def dot(a, b, dims):
    return lax.dot_general(a, b, (dims, ((), ())), preferred_element_type=F32)


def relay(source, target, held, sem, out_sem, n):
    return (
        pltpu.make_async_copy(source, held.at[n], sem.at[n]),
        pltpu.make_async_copy(held.at[n], target, out_sem.at[n]),
    )


def run_relays(relays):
    for inward, _ in relays:
        inward.start()
    for inward, outward in relays:
        inward.wait()
        outward.start()
    for _, outward in relays:
        outward.wait()


def collect_kernel(at_ref, *refs):
    ins, outs, (held, sem, out_sem) = refs[:16], refs[16:18], refs[18:]
    copies = []
    for state in range(2):
        own = at_ref[2] if state == 0 else at_ref[0]
        for n, (plane, distance) in enumerate([(p, d) for p in range(2) for d in range(4)]):
            where = outs[state].at[lax.rem(plane + at_ref[1], 2), lax.rem(own + distance, 4)]
            copies.append(relay(ins[8 * state + n], where, held, sem, out_sem, 8 * state + n))
    run_relays(copies)


def collect(at, blocks):
    shape = jax.ShapeDtypeStruct((2, 4) + blocks[0].shape, blocks[0].dtype)
    return pl.pallas_call(
        collect_kernel,
        out_shape=(shape,) * 2,
        in_specs=[pl.BlockSpec(memory_space=pltpu.SMEM)] + [pl.BlockSpec(memory_space=pl.ANY)] * 16,
        out_specs=(pl.BlockSpec(memory_space=pl.ANY),) * 2,
        scratch_shapes=[
            pltpu.VMEM((16,) + blocks[0].shape, blocks[0].dtype),
            pltpu.SemaphoreType.DMA((16,)),
            pltpu.SemaphoreType.DMA((16,)),
        ],
        compiler_params=pltpu.CompilerParams(vmem_limit_bytes=VMEM_LIMIT),
        cost_estimate=pl.CostEstimate(flops=0, bytes_accessed=8 << 20, transcendentals=0),
        name="collect",
    )(at, *blocks)


def around(near, other, axis):
    near_1, near_3 = hop(near, axis, -1), hop(near, axis, 1)
    other_3, other_1 = hop(other, axis, 1), hop(other, axis, -1)
    near_2 = hop(near_1, axis, -1)
    other_2 = hop(other_3, axis, 1)
    return [near, near_1, near_2, near_3, other, other_1, other_2, other_3]


def halves_kernel(*refs):
    outs, (held, sem, out_sem) = refs[-7:-3], refs[-3:]
    parts = [(n, z) for n in range(4) for z in range(4)]
    run_relays([relay(refs[n].at[n % 2, z], outs[n].at[z], held, sem, out_sem, 4 * n + z) for n, z in parts])


def halves(blocks, before):
    shape = jax.ShapeDtypeStruct(blocks[0].shape[1:], blocks[0].dtype)
    return pl.pallas_call(
        halves_kernel,
        out_shape=(shape,) * 4,
        in_specs=[pl.BlockSpec(memory_space=pl.ANY)] * (4 + len(before)),
        out_specs=(pl.BlockSpec(memory_space=pl.ANY),) * 4,
        scratch_shapes=[
            pltpu.VMEM((16,) + blocks[0].shape[2:], blocks[0].dtype),
            pltpu.SemaphoreType.DMA((16,)),
            pltpu.SemaphoreType.DMA((16,)),
        ],
        compiler_params=pltpu.CompilerParams(vmem_limit_bytes=VMEM_LIMIT),
        cost_estimate=pl.CostEstimate(flops=0, bytes_accessed=8 << 20, transcendentals=0),
        name="halves",
    )(*blocks, *before)


def gather_site(at, rows, before):
    first, second = rows[0], rows[1]
    first_other, second_other = hop(first, "x", 1), hop(second, "x", 1)
    a, b = collect(at, around(first, first_other, "z") + around(second, second_other, "y"))
    right_a, left_a, right_b, left_b = hop(a, "y", -1), hop(a, "y", 1), hop(b, "z", -1), hop(b, "z", 1)
    to_left_a, to_right_a, to_left_b, to_right_b = halves((right_a, left_a, right_b, left_b), before)
    return [
        *(a, right_a, left_a, hop(to_left_a, "y", -1), hop(to_right_a, "y", 1)),
        *(b, right_b, left_b, hop(to_left_b, "z", -1), hop(to_right_b, "z", 1)),
    ]


def site_copies(at_ref, blocks, buffer, sem, column, tile):
    made = []
    columns = pl.ds(pl.multiple_of(column, tile), tile)
    for x in range(2):
        for distance, place in ((0, 0), (1, 1), (3, 2), (2, 3 + x)):
            y, z = lax.rem(at_ref[0] + distance, 4), lax.rem(at_ref[2] + distance, 4)
            a, b = (ref if distance == 2 else ref.at[x] for ref in (blocks[place], blocks[5 + place]))
            n = 4 * x + distance
            made.append(pltpu.make_async_copy(a.at[:, :, columns], buffer.at[y, x, :, 0], sem.at[n]))
            made.append(pltpu.make_async_copy(b.at[:, :, columns], buffer.at[:, x, z, 1], sem.at[8 + n]))
    return made


def bond_kernel(r_ref, b_ref, o_ref):
    rows = o_ref.shape[1]
    full = dot(r_ref[...], b_ref[...], ((1,), (1,)))
    low = lax.broadcasted_iota(jnp.int32, (rows, 128), 1) < 64
    for j in range(o_ref.shape[0] // 2):
        for w in range(full.shape[0] // rows // 2):
            a = full[2 * w * rows : (2 * w + 1) * rows, 128 * j : 128 * j + 128]
            b = full[(2 * w + 1) * rows : (2 * w + 2) * rows, 128 * j : 128 * j + 128]
            lanes = pl.ds(128 * w, 128)
            o_ref[2 * j, :, lanes] = jnp.where(low, a, pltpu.roll(b, 64, 1)).astype(BF16)
            o_ref[2 * j + 1, :, lanes] = jnp.where(low, pltpu.roll(a, 64, 1), b).astype(BF16)


def bond_right(right_next, bond):
    w, rows, c = right_next.shape
    k = bond.shape[0]
    tile = 256
    return pl.pallas_call(
        bond_kernel,
        out_shape=jax.ShapeDtypeStruct((k // 64, rows, w * 64), BF16),
        grid=(k // tile,),
        in_specs=[
            pl.BlockSpec((w * rows, c), lambda i: (0, 0)),
            pl.BlockSpec((tile, c), lambda i: (i, 0)),
        ],
        out_specs=pl.BlockSpec((tile // 64, rows, w * 64), lambda i: (i, 0, 0)),
        compiler_params=pltpu.CompilerParams(vmem_limit_bytes=VMEM_LIMIT),
        cost_estimate=pl.CostEstimate(flops=2 * w * rows * c * k, bytes_accessed=12 << 20, transcendentals=0),
        name="bond_right",
    )(right_next.reshape(w * rows, c), bond)


def stacked(refs):
    return jnp.concatenate([ref[...].reshape(-1, ref.shape[-1]) for ref in refs], 0)


def begin_kernel(at_ref, first_ref, second_ref, *refs):
    blocks, h_ref, left_ref = refs[:6], refs[6], refs[7]

    @pl.when(pl.program_id(0) == 0)
    def _():
        for t, (source, own) in enumerate(((first_ref, at_ref[0]), (second_ref, at_ref[2]))):
            for n, distance in enumerate((0, 1, 3)):
                start = pl.multiple_of(512 * lax.rem(own + distance, 4), 512)
                left_ref[t, :, 512 * n : 512 * (n + 1)] = source[:, pl.ds(start, 512)]

    for t in range(2):
        h_ref[t] = dot(left_ref[t], stacked(blocks[3 * t : 3 * t + 3]), ((1,), (0,)))


def begin(at, first, second, blocks):
    rows, k = first.shape
    columns, tile = blocks[0].shape[-1], 256
    whole = pl.BlockSpec((rows, k), lambda i: (0, 0))
    return pl.pallas_call(
        begin_kernel,
        out_shape=jax.ShapeDtypeStruct((2, rows, columns), F32),
        grid=(columns // tile,),
        in_specs=[pl.BlockSpec(memory_space=pltpu.SMEM), whole, whole]
        + [pl.BlockSpec((2, 4, 64, tile), lambda i: (0, 0, 0, i))] * 6,
        out_specs=pl.BlockSpec((2, rows, tile), lambda i: (0, 0, i)),
        scratch_shapes=[pltpu.VMEM((2, rows, 3 * k // 4), BF16)],
        compiler_params=pltpu.CompilerParams(vmem_limit_bytes=VMEM_LIMIT),
        cost_estimate=pl.CostEstimate(flops=3 * rows * k * columns, bytes_accessed=24 << 20, transcendentals=0),
        name="begin",
    )(at, first, second, *blocks)


def hold(value, *before):
    anywhere = pl.BlockSpec(memory_space=pl.ANY)
    return pl.pallas_call(
        lambda *refs: None,
        out_shape=jax.ShapeDtypeStruct(value.shape, value.dtype),
        in_specs=[anywhere] * (1 + len(before)),
        out_specs=anywhere,
        input_output_aliases={0: 0},
        name="hold",
    )(value, *before)


def absorb_kernel(at_ref, m_ref, first_ref, second_ref, part_ref, *refs):
    blocks, o_ref, left_ref, h_ref = refs[:4], *refs[4:]
    w, tile = o_ref.shape[1], part_ref.shape[-1]
    rows = first_ref.shape[0] // w

    @pl.when(pl.program_id(0) == 0)
    def _():
        for t, (source, own) in enumerate(((first_ref, at_ref[0]), (second_ref, at_ref[2]))):
            left_ref[t] = source[:, pl.ds(pl.multiple_of(512 * lax.rem(own + 2, 4), 512), 512)]

    for t in range(2):
        h_ref[t] = part_ref[t] + dot(left_ref[t], stacked(blocks[2 * t : 2 * t + 2]), ((1,), (0,)))
    for v in range(w):
        sums = []
        for s in range(2):
            total = None
            for u in range(w):
                for t in range(2):
                    term = m_ref[((u * w + v) * 2 + s) * 2 + t] * h_ref[t, u * rows : (u + 1) * rows, :]
                    total = term if total is None else total + term
            sums.append(total)
        turned = jnp.concatenate(sums, 0).T
        o_ref[:, v] = turned.reshape(tile // 64, 64, 2 * rows).astype(BF16)


def absorb(at, mpo, first, second, part, blocks, w):
    rows, k = first.shape
    columns, tile = blocks[0].shape[-1], 256
    scalars = pl.BlockSpec(memory_space=pltpu.SMEM)
    whole = pl.BlockSpec((rows, k), lambda i: (0, 0))
    return pl.pallas_call(
        absorb_kernel,
        out_shape=jax.ShapeDtypeStruct((columns // 64, w, 64, 2 * rows // w), BF16),
        grid=(columns // tile,),
        in_specs=[scalars, scalars, whole, whole, pl.BlockSpec((2, rows, tile), lambda i: (0, 0, i))]
        + [pl.BlockSpec((4, 64, tile), lambda i: (0, 0, i))] * 4,
        out_specs=pl.BlockSpec((tile // 64, w, 64, 2 * rows // w), lambda i: (i, 0, 0, 0)),
        scratch_shapes=[pltpu.VMEM((2, rows, k // 4), BF16), pltpu.VMEM((2, rows, tile), F32)],
        compiler_params=pltpu.CompilerParams(vmem_limit_bytes=VMEM_LIMIT),
        cost_estimate=pl.CostEstimate(flops=rows * k * columns, bytes_accessed=20 << 20, transcendentals=0),
        name="absorb",
    )(at, mpo.reshape(-1), first, second, part, *blocks)


def step_kernel(at_ref, c_ref, *refs):
    blocks, e_ref, t_ref = refs[:10], refs[10], refs[11]
    buffer, lhs_ref, sem, lhs_sem = refs[12:]
    parts, depth = c_ref.shape[0], c_ref.shape[2]
    tile = buffer.shape[-1]
    i, count = pl.program_id(0), pl.num_programs(0)

    def copies(step):
        slot = lax.rem(step, 2)
        return site_copies(at_ref, blocks, buffer.at[slot], sem.at[slot], step * tile, tile)

    def sides():
        return [
            pltpu.make_async_copy(c_ref.at[p], lhs_ref.at[:, pl.ds(depth * p, depth)], lhs_sem.at[p])
            for p in range(parts)
        ]

    @pl.when(i == 0)
    def _():
        for copy in sides() + copies(i):
            copy.start()

    @pl.when(i + 1 < count)
    def _():
        for copy in copies(i + 1):
            copy.start()

    @pl.when(i == 0)
    def _():
        for copy in sides():
            copy.wait()

    for copy in copies(i):
        copy.wait()
    env = dot(lhs_ref[...], buffer[lax.rem(i, 2)].reshape(lhs_ref.shape[1], tile), ((1,), (0,)))
    e_ref[...] = env.astype(BF16)
    t_ref[...] = env.T.astype(BF16)


def step(at, carried, site):
    parts, rows, depth = carried.shape
    columns, tile = site[0].shape[-1], 256
    anywhere = pl.BlockSpec(memory_space=pl.ANY)
    return pl.pallas_call(
        step_kernel,
        out_shape=(jax.ShapeDtypeStruct((rows, columns), BF16), jax.ShapeDtypeStruct((columns, rows), BF16)),
        grid=(columns // tile,),
        in_specs=[pl.BlockSpec(memory_space=pltpu.SMEM)] + [anywhere] * 11,
        out_specs=(pl.BlockSpec((rows, tile), lambda i: (0, i)), pl.BlockSpec((tile, rows), lambda i: (i, 0))),
        scratch_shapes=[
            pltpu.VMEM((2, 4, 2, 4, 2, 64, tile), BF16),
            pltpu.VMEM((rows, parts * depth), BF16),
            pltpu.SemaphoreType.DMA((2, 16)),
            pltpu.SemaphoreType.DMA((parts,)),
        ],
        compiler_params=pltpu.CompilerParams(vmem_limit_bytes=VMEM_LIMIT),
        cost_estimate=pl.CostEstimate(flops=2 * rows * columns * parts * depth, bytes_accessed=24 << 20, transcendentals=0),
        name="step",
    )(at, carried, *site)


def terms_kernel(distances, at_ref, t_ref, b_ref, *outs):
    half = b_ref.shape[1] // 2
    n = len(distances)
    for m, distance in enumerate(distances):
        y, z = lax.rem(at_ref[0] + distance, 4), lax.rem(at_ref[2] + distance, 4)
        for side in range(2):
            for part in range(2):
                if side == 0:
                    rows = t_ref[pl.ds(2 * y + part, 1), :].reshape(256, -1)
                else:
                    rows = t_ref[4 * part : 4 * part + 4, pl.ds(z, 1)].reshape(256, -1)
                columns = b_ref[:, half * side : half * (side + 1)]
                outs[2 * n * side + 2 * m + part][...] = dot(rows, columns, ((1,), (0,))).astype(BF16)


def terms(distances, at, turned, bond):
    depth, columns = bond.shape
    half = columns // 2
    vmem = pl.BlockSpec(memory_space=pltpu.VMEM)
    count = 4 * len(distances)
    return pl.pallas_call(
        lambda *refs: terms_kernel(distances, *refs),
        out_shape=(jax.ShapeDtypeStruct((256, half), BF16),) * count,
        in_specs=[pl.BlockSpec(memory_space=pltpu.SMEM), vmem, vmem],
        out_specs=(vmem,) * count,
        compiler_params=pltpu.CompilerParams(vmem_limit_bytes=24 << 20),
        cost_estimate=pl.CostEstimate(flops=count * 2 * 256 * half * depth, bytes_accessed=count << 19, transcendentals=0),
        name="terms_%d" % len(distances),
    )(at, turned.reshape(8, 4, 64, depth), bond)


def add(*terms):
    total = terms[0].astype(F32)
    for term in terms[1:]:
        total = total + term.astype(F32)
    return total.astype(BF16)


def sum_line(far, right, left, own, axis):
    up, down = hop(far[0], axis, 1), hop(far[1], axis, -1)
    right = hop(jnp.stack([add(right[0], up), right[1]]), axis, 1)
    left = hop(jnp.stack([left[0], add(left[1], down)]), axis, -1)
    return add(jnp.stack(own), right, left)


def sum_short(blocks, axis):
    own = lax.axis_index(axis)
    right, far, left, mine = (lax.dynamic_index_in_dim(blocks, (own + d) % 4, 0, keepdims=False) for d in (1, 2, 3, 0))
    return add(mine, hop(right, axis, 1), hop(left, axis, -1), hop(far, axis, 2))


def scatter_image(far, rest):
    half = far[0].shape[-1]
    a = sum_line(far[:2], rest[0:2], rest[2:4], rest[4:6], "y")
    b = sum_line(far[2:], rest[6:8], rest[8:10], rest[10:12], "z")
    a = sum_short(a.reshape(2, 4, 64, half).transpose(1, 0, 2, 3), "z")
    b = sum_short(b.reshape(4, 2, 64, half), "y")
    both = jnp.concatenate([a, b], 2)
    own = lax.axis_index("x")
    theirs = hop(lax.dynamic_index_in_dim(both, 1 - own, 0, keepdims=False), "x", 1)
    return add(lax.dynamic_index_in_dim(both, own, 0, keepdims=False), theirs)


def local(env_left, site_tensor, mpo_tensor, env_right, bond_tensor):
    sector = ("y", "x", "z")
    at = jnp.stack([lax.axis_index(name) for name in sector]).astype(jnp.int32)
    route = [((i + 1) % 4, i) for i in range(4)]
    right_next = lax.ppermute(env_right, "region", route)[0]
    bond = bond_right(right_next, bond_tensor[0])
    w, rows, k = env_left.shape[1:]
    first = env_left.reshape(w * rows, k)
    second = first.reshape(w * rows, 4, 2, 4, 64).transpose(0, 3, 2, 1, 4).reshape(w * rows, k)
    site = gather_site(at, site_tensor[0].transpose(1, 0, 2), (bond, second))
    near, far = site[0:3] + site[5:8], site[3:5] + site[8:10]
    part = begin(at, first, second, near)
    bond = hold(bond, part, *site)
    bond = lax.all_to_all(bond, sector, split_axis=0, concat_axis=0, tiled=True)
    carried = absorb(at, mpo_tensor[0], first, second, part, far, w)
    carried = lax.all_to_all(carried, sector, split_axis=0, concat_axis=0, tiled=True)
    parts, w, columns, depth = carried.shape
    env_new, turned = step(at, carried.reshape(parts, w * columns, depth), site)
    bond = bond.reshape(-1, bond.shape[-1]).T
    far_terms = terms((2,), at, turned, bond)
    rest_terms = terms((1, 3, 0), at, turned, bond)
    return (env_new.reshape(1, w, columns, -1), scatter_image(far_terms, rest_terms)[None])


def solution(mesh):
    fine = Mesh(mesh.devices.reshape(4, 4, 2, 4), ("region", "y", "x", "z"))
    sector = ("y", "x", "z")
    return jax.shard_map(
        local,
        mesh=fine,
        in_specs=(
            P("region", None, sector, None),
            P("region", sector, None, None),
            P("region", None, None, None, None),
            P("region", None, sector, None),
            P("region", None, None),
        ),
        out_specs=(P("region", None, sector, None), P("region", sector, None)),
        check_vma=False,
    )
```

```python
import jax
import jax.numpy as jnp
from jax import lax
from jax.experimental import pallas as pl
from jax.experimental.pallas import tpu as pltpu
from jax.sharding import Mesh, PartitionSpec as P

F32, BF16 = jnp.float32, jnp.bfloat16
VMEM_LIMIT = 60 << 20


def hop(block, axis, distance):
    n = lax.axis_size(axis)
    return lax.ppermute(block, axis, [(i, (i + distance) % n) for i in range(n)])


def dot(a, b, dims):
    return lax.dot_general(a, b, (dims, ((), ())), preferred_element_type=F32)


def relay(source, target, held, sem, out_sem, n):
    return (
        pltpu.make_async_copy(source, held.at[n], sem.at[n]),
        pltpu.make_async_copy(held.at[n], target, out_sem.at[n]),
    )


def run_relays(relays):
    for inward, _ in relays:
        inward.start()
    for inward, outward in relays:
        inward.wait()
        outward.start()
    for _, outward in relays:
        outward.wait()


def collect_kernel(at_ref, *refs):
    ins, outs, (held, sem, out_sem) = refs[:16], refs[16:18], refs[18:]
    copies = []
    for state in range(2):
        own = at_ref[2] if state == 0 else at_ref[0]
        for n, (plane, distance) in enumerate([(p, d) for p in range(2) for d in range(4)]):
            where = outs[state].at[lax.rem(plane + at_ref[1], 2), lax.rem(own + distance, 4)]
            copies.append(relay(ins[8 * state + n], where, held, sem, out_sem, 8 * state + n))
    run_relays(copies)


def collect(at, blocks):
    shape = jax.ShapeDtypeStruct((2, 4) + blocks[0].shape, blocks[0].dtype)
    return pl.pallas_call(
        collect_kernel,
        out_shape=(shape,) * 2,
        in_specs=[pl.BlockSpec(memory_space=pltpu.SMEM)] + [pl.BlockSpec(memory_space=pl.ANY)] * 16,
        out_specs=(pl.BlockSpec(memory_space=pl.ANY),) * 2,
        scratch_shapes=[
            pltpu.VMEM((16,) + blocks[0].shape, blocks[0].dtype),
            pltpu.SemaphoreType.DMA((16,)),
            pltpu.SemaphoreType.DMA((16,)),
        ],
        compiler_params=pltpu.CompilerParams(vmem_limit_bytes=VMEM_LIMIT),
        cost_estimate=pl.CostEstimate(flops=0, bytes_accessed=8 << 20, transcendentals=0),
        name="collect",
    )(at, *blocks)


def around(near, other, axis):
    near_1, near_3 = hop(near, axis, -1), hop(near, axis, 1)
    other_3, other_1 = hop(other, axis, 1), hop(other, axis, -1)
    near_2 = hop(near_1, axis, -1)
    other_2 = hop(other_3, axis, 1)
    return [near, near_1, near_2, near_3, other, other_1, other_2, other_3]


def halves_kernel(*refs):
    outs, (held, sem, out_sem) = refs[-7:-3], refs[-3:]
    parts = [(n, z) for n in range(4) for z in range(4)]
    run_relays([relay(refs[n].at[n % 2, z], outs[n].at[z], held, sem, out_sem, 4 * n + z) for n, z in parts])


def halves(blocks, before):
    shape = jax.ShapeDtypeStruct(blocks[0].shape[1:], blocks[0].dtype)
    return pl.pallas_call(
        halves_kernel,
        out_shape=(shape,) * 4,
        in_specs=[pl.BlockSpec(memory_space=pl.ANY)] * (4 + len(before)),
        out_specs=(pl.BlockSpec(memory_space=pl.ANY),) * 4,
        scratch_shapes=[
            pltpu.VMEM((16,) + blocks[0].shape[2:], blocks[0].dtype),
            pltpu.SemaphoreType.DMA((16,)),
            pltpu.SemaphoreType.DMA((16,)),
        ],
        compiler_params=pltpu.CompilerParams(vmem_limit_bytes=VMEM_LIMIT),
        cost_estimate=pl.CostEstimate(flops=0, bytes_accessed=8 << 20, transcendentals=0),
        name="halves",
    )(*blocks, *before)


def gather_site(at, rows, before):
    first, second = rows[0], rows[1]
    first_other, second_other = hop(first, "x", 1), hop(second, "x", 1)
    a, b = collect(at, around(first, first_other, "z") + around(second, second_other, "y"))
    right_a, left_a, right_b, left_b = hop(a, "y", -1), hop(a, "y", 1), hop(b, "z", -1), hop(b, "z", 1)
    to_left_a, to_right_a, to_left_b, to_right_b = halves((right_a, left_a, right_b, left_b), before)
    return [
        *(a, right_a, left_a, hop(to_left_a, "y", -1), hop(to_right_a, "y", 1)),
        *(b, right_b, left_b, hop(to_left_b, "z", -1), hop(to_right_b, "z", 1)),
    ]


def site_copies(at_ref, blocks, buffer, sem, column, tile):
    made = []
    columns = pl.ds(pl.multiple_of(column, tile), tile)
    for x in range(2):
        for distance, place in ((0, 0), (1, 1), (3, 2), (2, 3 + x)):
            y, z = lax.rem(at_ref[0] + distance, 4), lax.rem(at_ref[2] + distance, 4)
            a, b = (ref if distance == 2 else ref.at[x] for ref in (blocks[place], blocks[5 + place]))
            n = 4 * x + distance
            made.append(pltpu.make_async_copy(a.at[:, :, columns], buffer.at[y, x, :, 0], sem.at[n]))
            made.append(pltpu.make_async_copy(b.at[:, :, columns], buffer.at[:, x, z, 1], sem.at[8 + n]))
    return made


def bond_kernel(r_ref, b_ref, o_ref):
    rows = o_ref.shape[1]
    full = dot(r_ref[...], b_ref[...], ((1,), (1,)))
    low = lax.broadcasted_iota(jnp.int32, (rows, 128), 1) < 64
    for j in range(o_ref.shape[0] // 2):
        for w in range(full.shape[0] // rows // 2):
            a = full[2 * w * rows : (2 * w + 1) * rows, 128 * j : 128 * j + 128]
            b = full[(2 * w + 1) * rows : (2 * w + 2) * rows, 128 * j : 128 * j + 128]
            lanes = pl.ds(128 * w, 128)
            o_ref[2 * j, :, lanes] = jnp.where(low, a, pltpu.roll(b, 64, 1)).astype(BF16)
            o_ref[2 * j + 1, :, lanes] = jnp.where(low, pltpu.roll(a, 64, 1), b).astype(BF16)


def bond_right(right_next, bond):
    w, rows, c = right_next.shape
    k = bond.shape[0]
    tile = 256
    return pl.pallas_call(
        bond_kernel,
        out_shape=jax.ShapeDtypeStruct((k // 64, rows, w * 64), BF16),
        grid=(k // tile,),
        in_specs=[
            pl.BlockSpec((w * rows, c), lambda i: (0, 0)),
            pl.BlockSpec((tile, c), lambda i: (i, 0)),
        ],
        out_specs=pl.BlockSpec((tile // 64, rows, w * 64), lambda i: (i, 0, 0)),
        compiler_params=pltpu.CompilerParams(vmem_limit_bytes=VMEM_LIMIT),
        cost_estimate=pl.CostEstimate(flops=2 * w * rows * c * k, bytes_accessed=12 << 20, transcendentals=0),
        name="bond_right",
    )(right_next.reshape(w * rows, c), bond)


def stacked(refs):
    return jnp.concatenate([ref[...].reshape(-1, ref.shape[-1]) for ref in refs], 0)


def begin_kernel(at_ref, first_ref, second_ref, *refs):
    blocks, h_ref, left_ref = refs[:6], refs[6], refs[7]

    @pl.when(pl.program_id(0) == 0)
    def _():
        for t, (source, own) in enumerate(((first_ref, at_ref[0]), (second_ref, at_ref[2]))):
            for n, distance in enumerate((0, 1, 3)):
                start = pl.multiple_of(512 * lax.rem(own + distance, 4), 512)
                left_ref[t, :, 512 * n : 512 * (n + 1)] = source[:, pl.ds(start, 512)]

    for t in range(2):
        h_ref[t] = dot(left_ref[t], stacked(blocks[3 * t : 3 * t + 3]), ((1,), (0,)))


def begin(at, first, second, blocks):
    rows, k = first.shape
    columns, tile = blocks[0].shape[-1], 256
    whole = pl.BlockSpec((rows, k), lambda i: (0, 0))
    return pl.pallas_call(
        begin_kernel,
        out_shape=jax.ShapeDtypeStruct((2, rows, columns), F32),
        grid=(columns // tile,),
        in_specs=[pl.BlockSpec(memory_space=pltpu.SMEM), whole, whole]
        + [pl.BlockSpec((2, 4, 64, tile), lambda i: (0, 0, 0, i))] * 6,
        out_specs=pl.BlockSpec((2, rows, tile), lambda i: (0, 0, i)),
        scratch_shapes=[pltpu.VMEM((2, rows, 3 * k // 4), BF16)],
        compiler_params=pltpu.CompilerParams(vmem_limit_bytes=VMEM_LIMIT),
        cost_estimate=pl.CostEstimate(flops=3 * rows * k * columns, bytes_accessed=24 << 20, transcendentals=0),
        name="begin",
    )(at, first, second, *blocks)


def hold(value, *before):
    anywhere = pl.BlockSpec(memory_space=pl.ANY)
    return pl.pallas_call(
        lambda *refs: None,
        out_shape=jax.ShapeDtypeStruct(value.shape, value.dtype),
        in_specs=[anywhere] * (1 + len(before)),
        out_specs=anywhere,
        input_output_aliases={0: 0},
        name="hold",
    )(value, *before)


def absorb_kernel(at_ref, m_ref, first_ref, second_ref, part_ref, *refs):
    blocks, o_ref, left_ref, h_ref = refs[:4], *refs[4:]
    w, tile = o_ref.shape[1], part_ref.shape[-1]
    rows = first_ref.shape[0] // w

    @pl.when(pl.program_id(0) == 0)
    def _():
        for t, (source, own) in enumerate(((first_ref, at_ref[0]), (second_ref, at_ref[2]))):
            left_ref[t] = source[:, pl.ds(pl.multiple_of(512 * lax.rem(own + 2, 4), 512), 512)]

    for t in range(2):
        h_ref[t] = part_ref[t] + dot(left_ref[t], stacked(blocks[2 * t : 2 * t + 2]), ((1,), (0,)))
    for v in range(w):
        sums = []
        for s in range(2):
            total = None
            for u in range(w):
                for t in range(2):
                    term = m_ref[((u * w + v) * 2 + s) * 2 + t] * h_ref[t, u * rows : (u + 1) * rows, :]
                    total = term if total is None else total + term
            sums.append(total)
        turned = jnp.concatenate(sums, 0).T
        o_ref[:, v] = turned.reshape(tile // 64, 64, 2 * rows).astype(BF16)


def absorb(at, mpo, first, second, part, blocks, w):
    rows, k = first.shape
    columns, tile = blocks[0].shape[-1], 256
    scalars = pl.BlockSpec(memory_space=pltpu.SMEM)
    whole = pl.BlockSpec((rows, k), lambda i: (0, 0))
    return pl.pallas_call(
        absorb_kernel,
        out_shape=jax.ShapeDtypeStruct((columns // 64, w, 64, 2 * rows // w), BF16),
        grid=(columns // tile,),
        in_specs=[scalars, scalars, whole, whole, pl.BlockSpec((2, rows, tile), lambda i: (0, 0, i))]
        + [pl.BlockSpec((4, 64, tile), lambda i: (0, 0, i))] * 4,
        out_specs=pl.BlockSpec((tile // 64, w, 64, 2 * rows // w), lambda i: (i, 0, 0, 0)),
        scratch_shapes=[pltpu.VMEM((2, rows, k // 4), BF16), pltpu.VMEM((2, rows, tile), F32)],
        compiler_params=pltpu.CompilerParams(vmem_limit_bytes=63 << 20),
        cost_estimate=pl.CostEstimate(flops=rows * k * columns, bytes_accessed=20 << 20, transcendentals=0),
        name="absorb",
    )(at, mpo.reshape(-1), first, second, part, *blocks)


def step_kernel(at_ref, c_ref, *refs):
    blocks, e_ref, t_ref = refs[:10], refs[10], refs[11]
    buffer, lhs_ref, sem, lhs_sem = refs[12:]
    parts, depth = c_ref.shape[0], c_ref.shape[2]
    tile = buffer.shape[-1]
    i, count = pl.program_id(0), pl.num_programs(0)

    def copies(step):
        slot = lax.rem(step, 2)
        return site_copies(at_ref, blocks, buffer.at[slot], sem.at[slot], step * tile, tile)

    def sides():
        return [
            pltpu.make_async_copy(c_ref.at[p], lhs_ref.at[:, pl.ds(depth * p, depth)], lhs_sem.at[p])
            for p in range(parts)
        ]

    @pl.when(i == 0)
    def _():
        for copy in sides() + copies(i):
            copy.start()

    @pl.when(i + 1 < count)
    def _():
        for copy in copies(i + 1):
            copy.start()

    @pl.when(i == 0)
    def _():
        for copy in sides():
            copy.wait()

    for copy in copies(i):
        copy.wait()
    env = dot(lhs_ref[...], buffer[lax.rem(i, 2)].reshape(lhs_ref.shape[1], tile), ((1,), (0,)))
    e_ref[...] = env.astype(BF16)
    t_ref[...] = env.T.astype(BF16)


def step(at, carried, site):
    parts, rows, depth = carried.shape
    columns, tile = site[0].shape[-1], 256
    anywhere = pl.BlockSpec(memory_space=pl.ANY)
    return pl.pallas_call(
        step_kernel,
        out_shape=(jax.ShapeDtypeStruct((rows, columns), BF16), jax.ShapeDtypeStruct((columns, rows), BF16)),
        grid=(columns // tile,),
        in_specs=[pl.BlockSpec(memory_space=pltpu.SMEM)] + [anywhere] * 11,
        out_specs=(pl.BlockSpec((rows, tile), lambda i: (0, i)), pl.BlockSpec((tile, rows), lambda i: (i, 0))),
        scratch_shapes=[
            pltpu.VMEM((2, 4, 2, 4, 2, 64, tile), BF16),
            pltpu.VMEM((rows, parts * depth), BF16),
            pltpu.SemaphoreType.DMA((2, 16)),
            pltpu.SemaphoreType.DMA((parts,)),
        ],
        compiler_params=pltpu.CompilerParams(vmem_limit_bytes=VMEM_LIMIT),
        cost_estimate=pl.CostEstimate(flops=2 * rows * columns * parts * depth, bytes_accessed=24 << 20, transcendentals=0),
        name="step",
    )(at, carried, *site)


def terms_kernel(distances, at_ref, t_ref, b_ref, *outs):
    half = b_ref.shape[1] // 2
    n = len(distances)
    for m, distance in enumerate(distances):
        y, z = lax.rem(at_ref[0] + distance, 4), lax.rem(at_ref[2] + distance, 4)
        for side in range(2):
            for part in range(2):
                if side == 0:
                    rows = t_ref[pl.ds(2 * y + part, 1), :].reshape(256, -1)
                else:
                    rows = t_ref[4 * part : 4 * part + 4, pl.ds(z, 1)].reshape(256, -1)
                columns = b_ref[:, half * side : half * (side + 1)]
                outs[2 * n * side + 2 * m + part][...] = dot(rows, columns, ((1,), (0,))).astype(BF16)


def terms(distances, at, turned, bond):
    depth, columns = bond.shape
    half = columns // 2
    vmem = pl.BlockSpec(memory_space=pltpu.VMEM)
    count = 4 * len(distances)
    return pl.pallas_call(
        lambda *refs: terms_kernel(distances, *refs),
        out_shape=(jax.ShapeDtypeStruct((256, half), BF16),) * count,
        in_specs=[pl.BlockSpec(memory_space=pltpu.SMEM), vmem, vmem],
        out_specs=(vmem,) * count,
        compiler_params=pltpu.CompilerParams(vmem_limit_bytes=24 << 20),
        cost_estimate=pl.CostEstimate(flops=count * 2 * 256 * half * depth, bytes_accessed=count << 19, transcendentals=0),
        name="terms_%d" % len(distances),
    )(at, turned.reshape(8, 4, 64, depth), bond)


def add(*terms):
    total = terms[0].astype(F32)
    for term in terms[1:]:
        total = total + term.astype(F32)
    return total.astype(BF16)


def sum_line(far, right, left, own, axis):
    up, down = hop(far[0], axis, 1), hop(far[1], axis, -1)
    right = hop(jnp.stack([add(right[0], up), right[1]]), axis, 1)
    left = hop(jnp.stack([left[0], add(left[1], down)]), axis, -1)
    return add(jnp.stack(own), right, left)


def sum_short(blocks, axis):
    own = lax.axis_index(axis)
    right, far, left, mine = (lax.dynamic_index_in_dim(blocks, (own + d) % 4, 0, keepdims=False) for d in (1, 2, 3, 0))
    return add(mine, hop(right, axis, 1), hop(left, axis, -1), hop(far, axis, 2))


def scatter_image(far, rest):
    half = far[0].shape[-1]
    a = sum_line(far[:2], rest[0:2], rest[2:4], rest[4:6], "y")
    b = sum_line(far[2:], rest[6:8], rest[8:10], rest[10:12], "z")
    a = sum_short(a.reshape(2, 4, 64, half).transpose(1, 0, 2, 3), "z")
    b = sum_short(b.reshape(4, 2, 64, half), "y")
    both = jnp.concatenate([a, b], 2)
    own = lax.axis_index("x")
    theirs = hop(lax.dynamic_index_in_dim(both, 1 - own, 0, keepdims=False), "x", 1)
    return add(lax.dynamic_index_in_dim(both, own, 0, keepdims=False), theirs)


def local(env_left, site_tensor, mpo_tensor, env_right, bond_tensor):
    sector = ("y", "x", "z")
    at = jnp.stack([lax.axis_index(name) for name in sector]).astype(jnp.int32)
    route = [((i + 1) % 4, i) for i in range(4)]
    right_next = lax.ppermute(env_right, "region", route)[0]
    bond = bond_right(right_next, bond_tensor[0])
    w, rows, k = env_left.shape[1:]
    first = env_left.reshape(w * rows, k)
    second = first.reshape(w * rows, 4, 2, 4, 64).transpose(0, 3, 2, 1, 4).reshape(w * rows, k)
    site = gather_site(at, site_tensor[0].transpose(1, 0, 2), (bond, second))
    near, far = site[0:3] + site[5:8], site[3:5] + site[8:10]
    part = begin(at, first, second, near)
    bond = hold(bond, part, *site)
    bond = lax.all_to_all(bond, sector, split_axis=0, concat_axis=0, tiled=True)
    carried = absorb(at, mpo_tensor[0], first, second, part, far, w)
    carried = lax.all_to_all(carried, sector, split_axis=0, concat_axis=0, tiled=True)
    parts, w, columns, depth = carried.shape
    env_new, turned = step(at, carried.reshape(parts, w * columns, depth), site)
    bond = bond.reshape(-1, bond.shape[-1]).T
    far_terms = terms((2,), at, turned, bond)
    rest_terms = terms((1, 3, 0), at, turned, bond)
    return (env_new.reshape(1, w, columns, -1), scatter_image(far_terms, rest_terms)[None])


def solution(mesh):
    fine = Mesh(mesh.devices.reshape(4, 4, 2, 4), ("region", "y", "x", "z"))
    sector = ("y", "x", "z")
    return jax.shard_map(
        local,
        mesh=fine,
        in_specs=(
            P("region", None, sector, None),
            P("region", sector, None, None),
            P("region", None, None, None, None),
            P("region", None, sector, None),
            P("region", None, None),
        ),
        out_specs=(P("region", None, sector, None), P("region", sector, None)),
        check_vma=False,
    )
```
